32 devices in a mesh: modes: 16 (over z, x, core), gz: 2 (over y).
Axes of the slice: x: 2, y: 2, z: 4, core: 2. Of those that a mesh axis runs over, the one named last changes fastest.
Arguments:
- fields: float32 [288, 64, 4, 128], P('modes', None, 'gz'), may hold values from -6 to 6
- mean_coeff: float32 [64, 4, 128], P(None, 'gz'), may hold values from 0.5 to 4
- random_coeff: float32 [10, 64, 4, 128], P(None, None, 'gz'), may hold values from -2.5 to 2.5
- coupling: int32 [1606, 4], replicated, may hold values from 0 to 285, as said below
- mode_slots: int32 [286], replicated, may hold values from 0 to 287, as said below
Outputs:
- applied: float32 [288, 64, 4, 128], P('modes', None, 'gz')
The draws below stay inside these ranges and needn't reach their ends.
Inputs may be any that keep to these rules, and one draw needn't show every extreme that they name: `coupling`: each row couples a mode with itself under term 0, or a mode with the mode one higher in the degree of one variable under the term that belongs to that variable, in both orders; each of the 10 variables belongs to a different term of 1 to 10, in no particular assignment; every such pair appears exactly once, in no particular order; modes are numbered by total degree. `mode_slots`: the slots are distinct.
All inputs are finite; a program needn't handle non-finite values.
Results may differ from the reference program's by a relative error of at most 0.000082.
Values sent between devices are 32-bit elements; how exact they have to be, the bound alone decides.
A program may use at most 64 MiB of HBM per device.

```python
import math
import jax
import jax.numpy as jnp
import numpy as np
from jax import lax

NVAR = 10
CHAOS_MODES = 286
BAND_ROWS = 64
CELLS_ACROSS = 128
MODE_SLOT_TOTAL = 288
CELLS_DEPTH = 4


def chaos_table(count):
    indices = [[0] * count]
    for first_var in range(count):
        entry = [0] * count
        entry[first_var] += 1
        indices.append(entry)
    for first_var in range(count):
        for second_var in range(first_var, count):
            entry = [0] * count
            entry[first_var] += 1
            entry[second_var] += 1
            indices.append(entry)
    for first_var in range(count):
        for second_var in range(first_var, count):
            for third_var in range(second_var, count):
                entry = [0] * count
                entry[first_var] += 1
                entry[second_var] += 1
                entry[third_var] += 1
                indices.append(entry)
    lookup = {}
    for number, entry in enumerate(indices):
        lookup[tuple(entry)] = number
    row_list = [[number, number, 0, 0] for number in range(len(indices))]
    for number, entry in enumerate(indices):
        if sum(entry) < 3:
            for var_pos in range(count):
                raised = list(entry)
                raised[var_pos] += 1
                partner = lookup[tuple(raised)]
                row_list.append([number, partner, var_pos + 1, entry[var_pos]])
                row_list.append([partner, number, var_pos + 1, entry[var_pos]])
    return np.array(row_list, dtype=np.int32)


def draw_coupling(key, part):
    table = jnp.asarray(chaos_table(NVAR))
    term_key = jax.random.fold_in(key, 5)
    term_perm = jax.random.permutation(term_key, NVAR).astype(jnp.int32)
    old_terms = table[:, 2]
    safe_index = jnp.maximum(old_terms - 1, 0)
    new_terms = jnp.where(old_terms == 0, 0, term_perm[safe_index] + 1).astype(jnp.int32)
    table = jnp.stack([table[:, 0], table[:, 1], new_terms, table[:, 3]], axis=1)
    order = jax.random.permutation(key, table.shape[0])
    return table[order].astype(jnp.int32)


def draw_mode_slots(key, part):
    nested_key = jax.random.fold_in(key, 11)
    outer_key = jax.random.fold_in(key, 23)
    central_part = jax.random.permutation(nested_key, MODE_SLOT_TOTAL - 2).astype(jnp.int32)[:CHAOS_MODES - 2] + 1
    boundary_ends = jnp.array([0, MODE_SLOT_TOTAL - 1], dtype=jnp.int32)
    chosen = jnp.concatenate([boundary_ends, central_part])
    order = jax.random.permutation(outer_key, CHAOS_MODES)
    return chosen[order].astype(jnp.int32)


def level_of(key, extent, pieces, smallest, largest):
    def one(dim, parts):
        steps = jax.random.uniform(jax.random.fold_in(jax.random.fold_in(key, 6), dim), (parts,), jnp.float32, smallest / len(pieces), largest / len(pieces))
        return jnp.repeat(jnp.exp(steps), extent[dim] // parts).reshape((-1,) + (1,) * (len(extent) - dim - 1))

    loudness = one(*pieces[0])
    for cut in pieces[1:]:
        loudness = loudness * one(*cut)
    return loudness


def scatter_about(key, dims, scale, reach, cuts=(), kind=jnp.bfloat16):
    result = scale * jax.random.normal(key, dims, jnp.float32)
    if cuts:
        result = result * level_of(key, dims, cuts, -0.22, 0.18)
    return jnp.clip(result, -reach, reach).astype(kind)


def setup_inputs(seed: int = 0) -> dict:
    arg_keys = jax.random.split(jax.random.key(seed), 6)
    return {
        "fields": scatter_about(arg_keys[0], (MODE_SLOT_TOTAL, BAND_ROWS, CELLS_DEPTH, CELLS_ACROSS), 1.0, 6.0, ((0, 16), (2, 2)), jnp.float32),
        "mean_coeff": jnp.clip(jnp.exp(math.log(4.0) - 2.0794415 * jax.random.uniform(arg_keys[1], (BAND_ROWS, CELLS_DEPTH, CELLS_ACROSS), jnp.float32) ** level_of(arg_keys[1], (BAND_ROWS, CELLS_DEPTH, CELLS_ACROSS), ((1, 2),), -0.2, 0.2)), 0.5, 4.0),
        "random_coeff": scatter_about(arg_keys[2], (NVAR, BAND_ROWS, CELLS_DEPTH, CELLS_ACROSS), 0.4, 2.5, ((2, 2),), jnp.float32),
        "coupling": draw_coupling(jax.random.fold_in(arg_keys[5], 71), 0),
        "mode_slots": draw_mode_slots(jax.random.fold_in(arg_keys[5], 71), 0),
    }


def neighbour(values, axis_pos, offset):
    selector = [slice(None)] * values.ndim
    for position in range(values.ndim - 3, values.ndim):
        if position == axis_pos:
            selector[position] = slice(1 + offset, values.shape[position] - 1 + offset)
        else:
            selector[position] = slice(1, values.shape[position] - 1)
    return values[tuple(selector)]

def stencil_one(padded_field, padded_coef):
    value_here = neighbour(padded_field, 0, 0)
    coef_here = neighbour(padded_coef, 0, 0)
    summed = jnp.zeros(value_here.shape, jnp.float32)
    for axis_pos in range(3):
        for offset in (-1, 1):
            value_next = neighbour(padded_field, axis_pos, offset)
            coef_next = neighbour(padded_coef, axis_pos, offset)
            summed = summed + 0.5 * (coef_here + coef_next) * (value_here - value_next)
    return summed

def pair_weights(coupling):
    degree = coupling[:, 3].astype(jnp.float32)
    raw_weight = (degree + 1.0) / jnp.sqrt((2.0 * degree + 1.0) * (2.0 * degree + 3.0))
    return jnp.where(coupling[:, 2] == 0, jnp.ones_like(raw_weight), raw_weight)

def reference(fields, mean_coeff, random_coeff, coupling, mode_slots):
    coef = jnp.concatenate([mean_coeff[None], random_coeff], axis=0)
    weight = pair_weights(coupling)
    target = mode_slots[coupling[:, 0]].astype(jnp.int32)
    source = mode_slots[coupling[:, 1]].astype(jnp.int32)
    term_ids = coupling[:, 2].astype(jnp.int32)
    padding = ((0, 0), (1, 1), (1, 1), (1, 1))
    padded_fields = jnp.pad(fields, padding)
    padded_coef = jnp.pad(coef, padding)

    def accumulate(carry, entry):
        tgt_slot, src_slot, term_id, factor = entry
        source_field = lax.dynamic_index_in_dim(padded_fields, src_slot, 0, keepdims=False)
        term_coef = lax.dynamic_index_in_dim(padded_coef, term_id, 0, keepdims=False)
        image = stencil_one(source_field, term_coef)
        current = lax.dynamic_index_in_dim(carry, tgt_slot, 0, keepdims=False)
        carry = lax.dynamic_update_index_in_dim(carry, current + factor * image, tgt_slot, 0)
        return (carry, None)
    start = jnp.zeros(fields.shape, jnp.float32)
    applied, unused = lax.scan(accumulate, start, (target, source, term_ids, weight))
    return applied
```

```python
import functools

import jax
import jax.numpy as jnp
from jax import lax
from jax.experimental import pallas as pl
from jax.experimental.pallas import tpu as pltpu
from jax.sharding import PartitionSpec as P

ACCS = 4
UNROLL = 8


def turn(value, shift, axis):
    size = value.shape[axis]
    shift %= size
    if shift == 0:
        return value
    low = lax.slice_in_dim(value, size - shift, size, axis=axis)
    high = lax.slice_in_dim(value, 0, size - shift, axis=axis)
    return jnp.concatenate([low, high], axis=axis)


def send_order(count):
    half = count // 2
    return sorted(range(1, count), key=lambda d: (abs(d - half), d))


def groups(own, parts):
    per = -(-own // parts)
    return per, [min(j * per, own - per) for j in range(parts)]


def barrier_with_peers(peers_modes, peers_gz):
    me, layer = lax.axis_index("modes"), lax.axis_index("gz")
    barrier = pltpu.get_barrier_semaphore()

    @pl.loop(1, peers_modes)
    def _(step):
        pl.semaphore_signal(
            barrier, inc=1, device_id=(lax.rem(me + step, peers_modes), layer),
            device_id_type=pl.DeviceIdType.MESH)

    @pl.loop(1, peers_gz)
    def _(step):
        pl.semaphore_signal(
            barrier, inc=1, device_id=(me, lax.rem(layer + step, peers_gz)),
            device_id_type=pl.DeviceIdType.MESH)

    pl.semaphore_wait(barrier, peers_modes + peers_gz - 2)


def spread_kernel(n, g, rows, depth, fields, coef, main, ylo, yhi, zlo, zhi, clo, chi,
                  ylo_out, yhi_out, zlo_out, zhi_out,
                  own_sem, send_sem, recv_sem, halo_send, halo_recv, coef_send, coef_recv):
    me, layer = lax.axis_index("modes"), lax.axis_index("gz")
    own = fields.shape[0]
    lines = rows * depth
    mesh_id = pl.DeviceIdType.MESH
    has = (me > 0, me < n - 1, layer > 0, layer < g - 1)
    to = ((me - 1, layer), (me + 1, layer), (me, layer - 1), (me, layer + 1))
    packed = (ylo_out, yhi_out, zlo_out, zhi_out)
    landing = (yhi, ylo, zhi, zlo)
    barrier_with_peers(n, g)

    def block_copy(step):
        target = lax.rem(me + step, n)
        return pltpu.make_async_remote_copy(
            src_ref=fields.at[:, target], dst_ref=main.at[me],
            send_sem=send_sem.at[step], recv_sem=recv_sem.at[step],
            device_id=(target, layer), device_id_type=mesh_id)

    def coef_copy(side):
        return pltpu.make_async_remote_copy(
            src_ref=coef, dst_ref=(chi, clo)[side - 2],
            send_sem=coef_send.at[side - 2], recv_sem=coef_recv.at[side - 2],
            device_id=to[side], device_id_type=mesh_id)

    def halo_copy(side, source):
        return pltpu.make_async_remote_copy(
            src_ref=packed[side].at[source], dst_ref=landing[side].at[source],
            send_sem=halo_send.at[side, source], recv_sem=halo_recv.at[side, source],
            device_id=to[side], device_id_type=mesh_id)

    order = send_order(n)
    for step in order:
        block_copy(step).start()
    mine = pltpu.make_async_copy(fields.at[:, me], main.at[me], own_sem)
    mine.start()
    for side in (2, 3):
        @pl.when(has[side])
        def _():
            coef_copy(side).start()

    y_per, y_starts = groups(own, rows)
    z_per, z_starts = groups(own, depth)

    def pack(source):
        line = lax.broadcasted_iota(jnp.int32, (1, lines, 1), 1)
        for out, edge in ((ylo_out, 0), (yhi_out, rows - 1)):
            tile = None
            for j, start in enumerate(y_starts):
                part = turn(main[source, start:start + y_per], (j - edge) * depth, 1)
                tile = part if tile is None else jnp.where(line // depth == j, part, tile)
            out[source] = tile
        for out, edge in ((zlo_out, 0), (zhi_out, depth - 1)):
            tile = None
            for j, start in enumerate(z_starts):
                part = turn(main[source, start:start + z_per], j - edge, 1)
                tile = part if tile is None else jnp.where(line % depth == j, part, tile)
            out[source] = tile

    def send_halo(source):
        for side in range(4):
            @pl.when(has[side])
            def _():
                halo_copy(side, source).start()

    mine.wait()
    pack(me)
    previous = me
    for step in order:
        source = lax.rem(me + n - step, n)
        block_copy(step).wait_recv()
        send_halo(previous)
        pack(source)
        previous = source
    for step in order:
        block_copy(step).wait_send()
    send_halo(previous)
    for side in range(4):
        @pl.when(has[side])
        def _():
            @pl.loop(0, n)
            def _(source):
                halo_copy(side, source).wait_send()

        opposite = (1, 0, 3, 2)[side]

        @pl.when(has[opposite])
        def _():
            @pl.loop(0, n)
            def _(source):
                halo_copy(side, source).wait_recv()
    for side in (2, 3):
        @pl.when(has[side])
        def _():
            coef_copy(side).wait_send()

        @pl.when(has[5 - side])
        def _():
            coef_copy(side).wait_recv()


def mix_kernel(n, g, rows, depth, pairs, couple, weight, slots, main, ylo, yhi, zlo, zhi,
               coef, clo, chi, out, shifted, faces, acc):
    me, layer = lax.axis_index("modes"), lax.axis_index("gz")
    own = main.shape[1]
    lines = rows * depth
    lanes = main.shape[3]
    terms = coef.shape[0]
    line = lax.broadcasted_iota(jnp.int32, (1, lines, lanes), 1)
    lane = lax.broadcasted_iota(jnp.int32, (1, lines, lanes), 2)
    row, deep = line // depth, line % depth

    def x_shift(value, offset):
        moved = pltpu.roll(value, offset % lanes, 2)
        edge = 0 if offset == 1 else lanes - 1
        return jnp.where(lane == edge, 0.0, moved)

    centre = coef[:, depth:depth + lines, :]
    before, after = clo[:, depth:depth + lines, :], chi[:, depth:depth + lines, :]
    z_before = jnp.where(layer > 0, turn(before, 1 - depth, 1), 0.0)
    z_after = jnp.where(layer < g - 1, turn(after, depth - 1, 1), 0.0)
    around = (
        coef[:, 0:lines, :],
        coef[:, 2 * depth:2 * depth + lines, :],
        jnp.where(deep == 0, z_before, turn(centre, 1, 1)),
        jnp.where(deep == depth - 1, z_after, turn(centre, -1, 1)),
        x_shift(centre, 1),
        x_shift(centre, -1),
    )
    total = None
    for m, other in enumerate(around):
        face = 0.5 * (centre + other)
        faces[:, m + 1] = face
        total = face if total is None else total + face
    faces[:, 0] = total

    y_per, y_starts = groups(own, rows)
    z_per, z_starts = groups(own, depth)

    def spans(starts, per):
        seen = 0
        for j, start in enumerate(starts):
            yield j, seen, min(own, start + per), start
            seen = min(own, start + per)

    has = (me > 0, me < n - 1, layer > 0, layer < g - 1)

    @pl.loop(0, n)
    def _(source):
        base = source * own
        value = main[source]
        shifted[pl.ds(base, own), 0] = value
        shifted[pl.ds(base, own), 5] = x_shift(value, 1)
        shifted[pl.ds(base, own), 6] = x_shift(value, -1)

        def edge_pieces(ref, starts, per, wanted, unit, here):
            pieces = []
            for j, first, stop, start in spans(starts, per):
                if stop > first:
                    tile = ref[source, first - start:stop - start]
                    pieces.append(turn(tile, (wanted - j) * unit, 1))
            joined = pieces[0] if len(pieces) == 1 else jnp.concatenate(pieces, axis=0)
            return jnp.where(here, joined, 0.0)

        low = edge_pieces(ylo, y_starts, y_per, 0, depth, has[0])
        high = edge_pieces(yhi, y_starts, y_per, rows - 1, depth, has[1])
        shifted[pl.ds(base, own), 1] = jnp.where(row == 0, low, turn(value, depth, 1))
        shifted[pl.ds(base, own), 2] = jnp.where(row == rows - 1, high, turn(value, -depth, 1))
        near = edge_pieces(zlo, z_starts, z_per, 0, 1, has[2])
        far = edge_pieces(zhi, z_starts, z_per, depth - 1, 1, has[3])
        shifted[pl.ds(base, own), 3] = jnp.where(deep == 0, near, turn(value, 1, 1))
        shifted[pl.ds(base, own), 4] = jnp.where(deep == depth - 1, far, turn(value, -1, 1))
        for a in range(ACCS):
            acc[a, pl.ds(base, own)] = jnp.zeros_like(value)

    def add_row(p, a):
        target = slots[couple[p]]
        source = slots[couple[pairs + p]]
        term = couple[2 * pairs + p]
        image = faces[term, 0] * shifted[source, 0]
        first = faces[term, 1] * shifted[source, 1] + faces[term, 2] * shifted[source, 2]
        second = faces[term, 3] * shifted[source, 3] + faces[term, 4] * shifted[source, 4]
        third = faces[term, 5] * shifted[source, 5] + faces[term, 6] * shifted[source, 6]
        image = (image - first) - (second + third)
        acc[a, target] = acc[a, target] + weight[p] * image

    whole = pairs // UNROLL

    @pl.loop(0, whole)
    def _(block):
        for u in range(UNROLL):
            add_row(block * UNROLL + u, u % ACCS)

    for p in range(whole * UNROLL, pairs):
        add_row(p, p % ACCS)

    @pl.loop(0, n)
    def _(source):
        base = source * own
        result = acc[0, pl.ds(base, own)]
        for a in range(1, ACCS):
            result = result + acc[a, pl.ds(base, own)]
        out[source] = result


def collect_kernel(n, result, out, own_sem, send_sem, recv_sem):
    me, layer = lax.axis_index("modes"), lax.axis_index("gz")
    barrier_with_peers(n, 1)

    def block_copy(step):
        target = lax.rem(me + step, n)
        return pltpu.make_async_remote_copy(
            src_ref=result.at[target], dst_ref=out.at[:, me],
            send_sem=send_sem.at[step], recv_sem=recv_sem.at[step],
            device_id=(target, layer), device_id_type=pl.DeviceIdType.MESH)

    order = send_order(n)
    for step in order:
        block_copy(step).start()
    mine = pltpu.make_async_copy(result.at[me], out.at[:, me], own_sem)
    mine.start()
    mine.wait()
    for step in order:
        block_copy(step).wait_recv()
    for step in order:
        block_copy(step).wait_send()


def body(fields, mean_coeff, random_coeff, coupling, mode_slots):
    n, g = lax.axis_size("modes"), lax.axis_size("gz")
    own, row_total, depth, across = fields.shape
    rows = row_total // n
    lines = rows * depth
    f32 = jnp.float32
    vmem = pl.BlockSpec(memory_space=pltpu.VMEM)
    smem = pl.BlockSpec(memory_space=pltpu.SMEM)
    dma = pltpu.SemaphoreType.DMA

    coef = jnp.concatenate([mean_coeff[None], random_coeff], axis=0)
    coef = jnp.pad(coef, ((0, 0), (1, 1), (0, 0), (0, 0)))
    coef = lax.dynamic_slice_in_dim(coef, lax.axis_index("modes") * rows, rows + 2, 1)
    terms = coef.shape[0]
    coef = coef.reshape(terms, (rows + 2) * depth, across)

    degree = coupling[:, 3].astype(f32)
    raw = (degree + 1.0) / jnp.sqrt((2.0 * degree + 1.0) * (2.0 * degree + 3.0))
    weight = jnp.where(coupling[:, 2] == 0, jnp.ones_like(raw), raw)
    pairs = coupling.shape[0]
    couple = coupling[:, :3].T.reshape(-1)

    y_per, _ = groups(own, rows)
    z_per, _ = groups(own, depth)
    block = jax.ShapeDtypeStruct((n, own, lines, across), f32)
    y_pack = jax.ShapeDtypeStruct((n, y_per, lines, across), f32)
    z_pack = jax.ShapeDtypeStruct((n, z_per, lines, across), f32)
    coef_like = jax.ShapeDtypeStruct(coef.shape, f32)
    spread = pl.pallas_call(
        functools.partial(spread_kernel, n, g, rows, depth),
        out_shape=(block, y_pack, y_pack, z_pack, z_pack, coef_like, coef_like),
        in_specs=[vmem, vmem],
        out_specs=[vmem] * 7,
        scratch_shapes=[
            pltpu.VMEM(y_pack.shape, f32), pltpu.VMEM(y_pack.shape, f32),
            pltpu.VMEM(z_pack.shape, f32), pltpu.VMEM(z_pack.shape, f32),
            dma, dma((n,)), dma((n,)), dma((4, n)), dma((4, n)), dma((2,)), dma((2,)),
        ],
        compiler_params=pltpu.CompilerParams(collective_id=0, has_side_effects=True),
        name="spread",
    )
    main, ylo, yhi, zlo, zhi, clo, chi = spread(fields.reshape(own, n, lines, across), coef)

    mix = pl.pallas_call(
        functools.partial(mix_kernel, n, g, rows, depth, pairs),
        out_shape=block,
        in_specs=[smem, smem, smem] + [vmem] * 8,
        out_specs=vmem,
        scratch_shapes=[
            pltpu.VMEM((n * own, 7, lines, across), f32),
            pltpu.VMEM((terms, 7, lines, across), f32),
            pltpu.VMEM((ACCS, n * own, lines, across), f32),
        ],
        name="mix",
    )
    result = mix(couple, weight, mode_slots, main, ylo, yhi, zlo, zhi, coef, clo, chi)

    collect = pl.pallas_call(
        functools.partial(collect_kernel, n),
        out_shape=jax.ShapeDtypeStruct((own, n, lines, across), f32),
        in_specs=[vmem],
        out_specs=vmem,
        scratch_shapes=[dma, dma((n,)), dma((n,))],
        compiler_params=pltpu.CompilerParams(collective_id=1, has_side_effects=True),
        name="collect",
    )
    return collect(result).reshape(fields.shape)


def solution(mesh):
    in_specs = (
        P("modes", None, "gz", None),
        P(None, "gz", None),
        P(None, None, "gz", None),
        P(),
        P(),
    )
    out_specs = P("modes", None, "gz", None)
    return jax.shard_map(body, mesh=mesh, in_specs=in_specs, out_specs=out_specs, check_vma=False)
```

```python
import functools

import jax
import jax.numpy as jnp
from jax import lax
from jax.experimental import pallas as pl
from jax.experimental.pallas import tpu as pltpu
from jax.sharding import PartitionSpec as P

ACCS = 4
UNROLL = 22


def turn(value, shift, axis):
    size = value.shape[axis]
    shift %= size
    if shift == 0:
        return value
    low = lax.slice_in_dim(value, size - shift, size, axis=axis)
    high = lax.slice_in_dim(value, 0, size - shift, axis=axis)
    return jnp.concatenate([low, high], axis=axis)


def send_order(count):
    return sorted(range(1, count), key=lambda d: (min(d, count - d), d))


def groups(own, parts):
    per = -(-own // parts)
    return per, [min(j * per, own - per) for j in range(parts)]


def barrier_with_peers(peers_modes, peers_gz):
    me, layer = lax.axis_index("modes"), lax.axis_index("gz")
    barrier = pltpu.get_barrier_semaphore()

    @pl.loop(1, peers_modes)
    def _(step):
        pl.semaphore_signal(
            barrier, inc=1, device_id=(lax.rem(me + step, peers_modes), layer),
            device_id_type=pl.DeviceIdType.MESH)

    @pl.loop(1, peers_gz)
    def _(step):
        pl.semaphore_signal(
            barrier, inc=1, device_id=(me, lax.rem(layer + step, peers_gz)),
            device_id_type=pl.DeviceIdType.MESH)

    pl.semaphore_wait(barrier, peers_modes + peers_gz - 2)


def spread_kernel(n, g, rows, depth, couple, slots, table, fields, coef,
                  main, ylo, yhi, zlo, zhi, clo, chi, to_off, from_off, term_off, weight,
                  ylo_out, yhi_out, zlo_out, zhi_out,
                  own_sem, send_sem, recv_sem, halo_send, halo_recv, coef_send, coef_recv):
    me, layer = lax.axis_index("modes"), lax.axis_index("gz")
    own = fields.shape[0]
    lines = rows * depth
    mesh_id = pl.DeviceIdType.MESH
    has = (me > 0, me < n - 1, layer > 0, layer < g - 1)
    to = ((me - 1, layer), (me + 1, layer), (me, layer - 1), (me, layer + 1))
    packed = (ylo_out, yhi_out, zlo_out, zhi_out)
    landing = (yhi, ylo, zhi, zlo)
    barrier_with_peers(n, g)

    def block_copy(step):
        target = lax.rem(me + step, n)
        return pltpu.make_async_remote_copy(
            src_ref=fields.at[:, target], dst_ref=main.at[me],
            send_sem=send_sem.at[step], recv_sem=recv_sem.at[step],
            device_id=(target, layer), device_id_type=mesh_id)

    def coef_copy(side):
        return pltpu.make_async_remote_copy(
            src_ref=coef, dst_ref=(chi, clo)[side - 2],
            send_sem=coef_send.at[side - 2], recv_sem=coef_recv.at[side - 2],
            device_id=to[side], device_id_type=mesh_id)

    def halo_copy(side, source):
        return pltpu.make_async_remote_copy(
            src_ref=packed[side].at[source], dst_ref=landing[side].at[source],
            send_sem=halo_send.at[side, source], recv_sem=halo_recv.at[side, source],
            device_id=to[side], device_id_type=mesh_id)

    order = send_order(n)
    for step in order:
        block_copy(step).start()
    mine = pltpu.make_async_copy(fields.at[:, me], main.at[me], own_sem)
    mine.start()
    for side in (2, 3):
        @pl.when(has[side])
        def _():
            coef_copy(side).start()

    y_per, y_starts = groups(own, rows)
    z_per, z_starts = groups(own, depth)

    pairs = couple.shape[1]
    share = -(-pairs // n)

    def decode(part):
        @pl.loop(part * share, min(pairs, (part + 1) * share))
        def _(p):
            term = couple[2, p]
            to_off[p] = slots[couple[0, p]] * lines
            from_off[p] = slots[couple[1, p]] * (7 * lines)
            term_off[p] = term * (7 * lines)
            weight[p] = jnp.where(term == 0, jnp.float32(1.0), table[couple[3, p]])

    def pack(source):
        line = lax.broadcasted_iota(jnp.int32, (1, lines, 1), 1)
        for out, edge in ((ylo_out, 0), (yhi_out, rows - 1)):
            tile = None
            for j, start in enumerate(y_starts):
                part = turn(main[source, start:start + y_per], (j - edge) * depth, 1)
                tile = part if tile is None else jnp.where(line // depth == j, part, tile)
            out[source] = tile
        for out, edge in ((zlo_out, 0), (zhi_out, depth - 1)):
            tile = None
            for j, start in enumerate(z_starts):
                part = turn(main[source, start:start + z_per], j - edge, 1)
                tile = part if tile is None else jnp.where(line % depth == j, part, tile)
            out[source] = tile

    def send_halo(source):
        for side in range(4):
            @pl.when(has[side])
            def _():
                halo_copy(side, source).start()

    decode(0)
    mine.wait()
    pack(me)
    previous = me
    for part, step in enumerate(order):
        source = lax.rem(me + n - step, n)
        block_copy(step).wait_recv()
        send_halo(previous)
        pack(source)
        decode(part + 1)
        previous = source
    for step in order:
        block_copy(step).wait_send()
    send_halo(previous)
    for side in range(4):
        @pl.when(has[side])
        def _():
            @pl.loop(0, n)
            def _(source):
                halo_copy(side, source).wait_send()

        opposite = (1, 0, 3, 2)[side]

        @pl.when(has[opposite])
        def _():
            @pl.loop(0, n)
            def _(source):
                halo_copy(side, source).wait_recv()
    for side in (2, 3):
        @pl.when(has[side])
        def _():
            coef_copy(side).wait_send()

        @pl.when(has[5 - side])
        def _():
            coef_copy(side).wait_recv()


def mix_kernel(n, g, rows, depth, pairs, to_off, from_off, term_off, weight, main, ylo, yhi, zlo, zhi,
               coef, clo, chi, out, shifted, faces, acc):
    me, layer = lax.axis_index("modes"), lax.axis_index("gz")
    own = main.shape[1]
    lines = rows * depth
    lanes = main.shape[3]
    terms = coef.shape[0]
    line = lax.broadcasted_iota(jnp.int32, (1, lines, lanes), 1)
    lane = lax.broadcasted_iota(jnp.int32, (1, lines, lanes), 2)
    row, deep = line // depth, line % depth

    def x_shift(value, offset):
        moved = pltpu.roll(value, offset % lanes, 2)
        edge = 0 if offset == 1 else lanes - 1
        return jnp.where(lane == edge, 0.0, moved)

    centre = coef[:, depth:depth + lines, :]
    before, after = clo[:, depth:depth + lines, :], chi[:, depth:depth + lines, :]
    z_before = jnp.where(layer > 0, turn(before, 1 - depth, 1), 0.0)
    z_after = jnp.where(layer < g - 1, turn(after, depth - 1, 1), 0.0)
    around = (
        coef[:, 0:lines, :],
        coef[:, 2 * depth:2 * depth + lines, :],
        jnp.where(deep == 0, z_before, turn(centre, 1, 1)),
        jnp.where(deep == depth - 1, z_after, turn(centre, -1, 1)),
        x_shift(centre, 1),
        x_shift(centre, -1),
    )

    def put_faces(m, value):
        for k in range(terms):
            faces[(k * 7 + m) * lines:(k * 7 + m + 1) * lines, :] = value[k]

    total = None
    for m, other in enumerate(around):
        face = 0.5 * (centre + other)
        put_faces(m + 1, face)
        total = face if total is None else total + face
    put_faces(0, total)

    y_per, y_starts = groups(own, rows)
    z_per, z_starts = groups(own, depth)

    def spans(starts, per):
        seen = 0
        for j, start in enumerate(starts):
            yield j, seen, min(own, start + per), start
            seen = min(own, start + per)

    has = (me > 0, me < n - 1, layer > 0, layer < g - 1)

    def put(base, m, value):
        for i in range(own):
            start = pl.multiple_of(base * (7 * lines), lines) + (i * 7 + m) * lines
            shifted[pl.ds(start, lines), :] = value[i]

    @pl.loop(0, n)
    def _(source):
        base = source * own
        value = main[source]
        put(base, 0, value)
        put(base, 5, x_shift(value, 1))
        put(base, 6, x_shift(value, -1))

        def edge_pieces(ref, starts, per, wanted, unit, here):
            pieces = []
            for j, first, stop, start in spans(starts, per):
                if stop > first:
                    tile = ref[source, first - start:stop - start]
                    pieces.append(turn(tile, (wanted - j) * unit, 1))
            joined = pieces[0] if len(pieces) == 1 else jnp.concatenate(pieces, axis=0)
            return jnp.where(here, joined, 0.0)

        low = edge_pieces(ylo, y_starts, y_per, 0, depth, has[0])
        high = edge_pieces(yhi, y_starts, y_per, rows - 1, depth, has[1])
        put(base, 1, jnp.where(row == 0, low, turn(value, depth, 1)))
        put(base, 2, jnp.where(row == rows - 1, high, turn(value, -depth, 1)))
        near = edge_pieces(zlo, z_starts, z_per, 0, 1, has[2])
        far = edge_pieces(zhi, z_starts, z_per, depth - 1, 1, has[3])
        put(base, 3, jnp.where(deep == 0, near, turn(value, 1, 1)))
        put(base, 4, jnp.where(deep == depth - 1, far, turn(value, -1, 1)))
        for a in range(ACCS):
            acc[a, pl.ds(pl.multiple_of(base * lines, lines), own * lines), :] = jnp.zeros(
                (own * lines, lanes), jnp.float32)

    def tiles(ref, offset, index):
        return ref[pl.ds(pl.multiple_of(offset, lines) + index * lines, lines), :]

    def add_row(p, a):
        term, source, target = term_off[p], from_off[p], to_off[p]
        part = [tiles(faces, term, m) * tiles(shifted, source, m) for m in range(7)]
        image = (part[0] - (part[1] + part[2])) - ((part[3] + part[4]) + (part[5] + part[6]))
        here = pl.ds(pl.multiple_of(target, lines), lines)
        acc[a, here, :] = acc[a, here, :] + weight[p] * image

    whole = pairs // UNROLL

    @pl.loop(0, whole)
    def _(block):
        for u in range(UNROLL):
            add_row(block * UNROLL + u, u % ACCS)

    for p in range(whole * UNROLL, pairs):
        add_row(p, p % ACCS)

    @pl.loop(0, n)
    def _(source):
        here = pl.ds(pl.multiple_of(source * own * lines, lines), own * lines)
        result = acc[0, here, :]
        for a in range(1, ACCS):
            result = result + acc[a, here, :]
        out[source] = result


def store_kernel(source, out, held, into, back):
    count = source.shape[0]
    for i in range(count):
        pltpu.make_async_copy(source.at[i], held.at[i], into.at[i]).start()
    for i in range(count):
        pltpu.make_async_copy(source.at[i], held.at[i], into.at[i]).wait()
        pltpu.make_async_copy(held.at[i], out.at[i], back.at[i]).start()
    for i in range(count):
        pltpu.make_async_copy(held.at[i], out.at[i], back.at[i]).wait()


def collect_kernel(n, result, out, own_sem, send_sem, recv_sem):
    me, layer = lax.axis_index("modes"), lax.axis_index("gz")
    barrier_with_peers(n, 1)

    def block_copy(step):
        target = lax.rem(me + step, n)
        return pltpu.make_async_remote_copy(
            src_ref=result.at[target], dst_ref=out.at[:, me],
            send_sem=send_sem.at[step], recv_sem=recv_sem.at[step],
            device_id=(target, layer), device_id_type=pl.DeviceIdType.MESH)

    order = send_order(n)
    for step in order:
        block_copy(step).start()
    mine = pltpu.make_async_copy(result.at[me], out.at[:, me], own_sem)
    mine.start()
    mine.wait()
    for step in order:
        block_copy(step).wait_recv()
    for step in order:
        block_copy(step).wait_send()


def body(fields, mean_coeff, random_coeff, coupling, mode_slots):
    n, g = lax.axis_size("modes"), lax.axis_size("gz")
    own, row_total, depth, across = fields.shape
    rows = row_total // n
    lines = rows * depth
    f32 = jnp.float32
    vmem = pl.BlockSpec(memory_space=pltpu.VMEM)
    smem = pl.BlockSpec(memory_space=pltpu.SMEM)
    anywhere = pl.BlockSpec(memory_space=pl.ANY)
    dma = pltpu.SemaphoreType.DMA

    coef = jnp.concatenate([mean_coeff[None], random_coeff], axis=0)
    coef = jnp.pad(coef, ((0, 0), (1, 1), (0, 0), (0, 0)))
    coef = lax.dynamic_slice_in_dim(coef, lax.axis_index("modes") * rows, rows + 2, 1)
    terms = coef.shape[0]
    coef = coef.reshape(terms, (rows + 2) * depth, across)

    degree = jnp.arange(mode_slots.shape[0], dtype=jnp.int32).astype(f32)
    table = (degree + 1.0) / jnp.sqrt((2.0 * degree + 1.0) * (2.0 * degree + 3.0))
    couple = coupling.T
    pairs = couple.shape[1]

    y_per, _ = groups(own, rows)
    z_per, _ = groups(own, depth)
    block = jax.ShapeDtypeStruct((n, own, lines, across), f32)
    y_pack = jax.ShapeDtypeStruct((n, y_per, lines, across), f32)
    z_pack = jax.ShapeDtypeStruct((n, z_per, lines, across), f32)
    offsets = jax.ShapeDtypeStruct((pairs,), jnp.int32)
    coef_like = jax.ShapeDtypeStruct(coef.shape, f32)
    spread = pl.pallas_call(
        functools.partial(spread_kernel, n, g, rows, depth),
        out_shape=(block, y_pack, y_pack, z_pack, z_pack, coef_like, coef_like,
                   offsets, offsets, offsets, jax.ShapeDtypeStruct((pairs,), f32)),
        in_specs=[smem, smem, smem, anywhere, vmem],
        out_specs=[vmem] * 7 + [smem] * 4,
        scratch_shapes=[
            pltpu.VMEM(y_pack.shape, f32), pltpu.VMEM(y_pack.shape, f32),
            pltpu.VMEM(z_pack.shape, f32), pltpu.VMEM(z_pack.shape, f32),
            dma, dma((n,)), dma((n,)), dma((4, n)), dma((4, n)), dma((2,)), dma((2,)),
        ],
        compiler_params=pltpu.CompilerParams(collective_id=0, has_side_effects=True),
        name="spread",
    )
    received = spread(couple, mode_slots, table, fields.reshape(own, n, lines, across), coef)
    main, ylo, yhi, zlo, zhi, clo, chi, to_off, from_off, term_off, weight = received

    mix = pl.pallas_call(
        functools.partial(mix_kernel, n, g, rows, depth, pairs),
        out_shape=jax.ShapeDtypeStruct((n, own * lines, across), f32),
        in_specs=[smem] * 4 + [vmem] * 8,
        out_specs=vmem,
        scratch_shapes=[
            pltpu.VMEM((n * own * 7 * lines, across), f32),
            pltpu.VMEM((terms * 7 * lines, across), f32),
            pltpu.VMEM((ACCS, n * own * lines, across), f32),
        ],
        name="mix",
    )
    result = mix(to_off, from_off, term_off, weight, main, ylo, yhi, zlo, zhi, coef, clo, chi)

    collect = pl.pallas_call(
        functools.partial(collect_kernel, n),
        out_shape=jax.ShapeDtypeStruct((own, n, lines, across), f32),
        in_specs=[vmem],
        out_specs=vmem,
        scratch_shapes=[dma, dma((n,)), dma((n,))],
        compiler_params=pltpu.CompilerParams(collective_id=1, has_side_effects=True),
        name="collect",
    )
    local = (own, n, lines, across)
    store = pl.pallas_call(
        store_kernel,
        out_shape=jax.ShapeDtypeStruct(local, f32),
        in_specs=[anywhere],
        out_specs=anywhere,
        scratch_shapes=[pltpu.VMEM(local, f32), dma((own,)), dma((own,))],
        name="store",
    )
    return store(collect(result.reshape(block.shape))).reshape(fields.shape)


def solution(mesh):
    in_specs = (
        P("modes", None, "gz", None),
        P(None, "gz", None),
        P(None, None, "gz", None),
        P(),
        P(),
    )
    out_specs = P("modes", None, "gz", None)
    return jax.shard_map(body, mesh=mesh, in_specs=in_specs, out_specs=out_specs, check_vma=False)
```

```python
import functools

import jax
import jax.numpy as jnp
from jax import lax
from jax.experimental import pallas as pl
from jax.experimental.pallas import tpu as pltpu
from jax.sharding import PartitionSpec as P

ACCS = 2
UNROLL = 22


def turn(value, shift, axis):
    size = value.shape[axis]
    shift %= size
    if shift == 0:
        return value
    low = lax.slice_in_dim(value, size - shift, size, axis=axis)
    high = lax.slice_in_dim(value, 0, size - shift, axis=axis)
    return jnp.concatenate([low, high], axis=axis)


def step_plan(count):
    plane = max(p for p in range(1, count + 1) if count % p == 0 and p * p <= count)
    planes = count // plane
    far = sorted(range(1, planes), key=lambda d: (abs(d - planes // 2), d))
    near = [(0, j) for j in range(1, plane)]
    away = [(d, j) for d in far for j in range(plane)]
    return away + near, near + away, plane


def partner(me, step, count, plane, sign):
    planes = count // plane
    outer = lax.rem(me // plane + planes + sign * step[0], planes)
    inner = lax.rem(lax.rem(me, plane) + plane + sign * step[1], plane)
    return outer * plane + inner


def groups(own, parts):
    per = -(-own // parts)
    return per, [min(j * per, own - per) for j in range(parts)]


def barrier_with_peers(peers_modes, peers_gz):
    me, layer = lax.axis_index("modes"), lax.axis_index("gz")
    barrier = pltpu.get_barrier_semaphore()

    @pl.loop(1, peers_modes)
    def _(step):
        pl.semaphore_signal(
            barrier, inc=1, device_id=(lax.rem(me + step, peers_modes), layer),
            device_id_type=pl.DeviceIdType.MESH)

    @pl.loop(1, peers_gz)
    def _(step):
        pl.semaphore_signal(
            barrier, inc=1, device_id=(me, lax.rem(layer + step, peers_gz)),
            device_id_type=pl.DeviceIdType.MESH)

    pl.semaphore_wait(barrier, peers_modes + peers_gz - 2)


def spread_kernel(n, g, rows, depth, couple, slots, table, fields, coef,
                  main_out, ylo, yhi, zlo, zhi, clo, chi, to_off, from_off, term_off, weight,
                  main, ylo_out, yhi_out, zlo_out, zhi_out, out_sem,
                  own_sem, send_sem, recv_sem, halo_send, halo_recv, coef_send, coef_recv):
    me, layer = lax.axis_index("modes"), lax.axis_index("gz")
    own = fields.shape[0]
    lines = rows * depth
    mesh_id = pl.DeviceIdType.MESH
    has = (me > 0, me < n - 1, layer > 0, layer < g - 1)
    to = ((me - 1, layer), (me + 1, layer), (me, layer - 1), (me, layer + 1))
    packed = (ylo_out, yhi_out, zlo_out, zhi_out)
    landing = (yhi, ylo, zhi, zlo)
    barrier_with_peers(n, g)

    sends, waits, plane = step_plan(n)

    def block_copy(step):
        target = partner(me, step, n, plane, 1)
        slot = step[0] * plane + step[1]
        return pltpu.make_async_remote_copy(
            src_ref=fields.at[:, target], dst_ref=main.at[me],
            send_sem=send_sem.at[slot], recv_sem=recv_sem.at[slot],
            device_id=(target, layer), device_id_type=mesh_id)

    def coef_copy(side):
        return pltpu.make_async_remote_copy(
            src_ref=coef, dst_ref=(chi, clo)[side - 2],
            send_sem=coef_send.at[side - 2], recv_sem=coef_recv.at[side - 2],
            device_id=to[side], device_id_type=mesh_id)

    def halo_copy(side, source):
        return pltpu.make_async_remote_copy(
            src_ref=packed[side].at[source], dst_ref=landing[side].at[source],
            send_sem=halo_send.at[side, source], recv_sem=halo_recv.at[side, source],
            device_id=to[side], device_id_type=mesh_id)

    for step in sends:
        block_copy(step).start()
    mine = pltpu.make_async_copy(fields.at[:, me], main.at[me], own_sem)
    mine.start()
    for side in (2, 3):
        @pl.when(has[side])
        def _():
            coef_copy(side).start()

    y_per, y_starts = groups(own, rows)
    z_per, z_starts = groups(own, depth)

    pairs = couple.shape[1]
    share = -(-pairs // n)

    def decode(part):
        @pl.loop(part * share, min(pairs, (part + 1) * share))
        def _(p):
            term = couple[2, p]
            to_off[p] = slots[couple[0, p]] * lines
            from_off[p] = slots[couple[1, p]] * (7 * lines)
            term_off[p] = term * (7 * lines)
            weight[p] = jnp.where(term == 0, jnp.float32(1.0), table[couple[3, p]])

    def pack(source):
        line = lax.broadcasted_iota(jnp.int32, (1, lines, 1), 1)
        for out, edge in ((ylo_out, 0), (yhi_out, rows - 1)):
            tile = None
            for j, start in enumerate(y_starts):
                part = turn(main[source, start:start + y_per], (j - edge) * depth, 1)
                tile = part if tile is None else jnp.where(line // depth == j, part, tile)
            out[source] = tile
        for out, edge in ((zlo_out, 0), (zhi_out, depth - 1)):
            tile = None
            for j, start in enumerate(z_starts):
                part = turn(main[source, start:start + z_per], j - edge, 1)
                tile = part if tile is None else jnp.where(line % depth == j, part, tile)
            out[source] = tile

    def keep(source):
        return pltpu.make_async_copy(main.at[source], main_out.at[source], out_sem.at[source])

    def send_halo(source):
        for side in range(4):
            @pl.when(has[side])
            def _():
                halo_copy(side, source).start()

    decode(0)
    mine.wait()
    keep(me).start()
    pack(me)
    previous = me
    for part, step in enumerate(waits):
        source = partner(me, step, n, plane, -1)
        block_copy(step).wait_recv()
        keep(source).start()
        send_halo(previous)
        pack(source)
        decode(part + 1)
        previous = source
    for step in sends:
        block_copy(step).wait_send()
    send_halo(previous)

    @pl.loop(0, n)
    def _(source):
        keep(source).wait()

    for side in range(4):
        @pl.when(has[side])
        def _():
            @pl.loop(0, n)
            def _(source):
                halo_copy(side, source).wait_send()

        opposite = (1, 0, 3, 2)[side]

        @pl.when(has[opposite])
        def _():
            @pl.loop(0, n)
            def _(source):
                halo_copy(side, source).wait_recv()
    for side in (2, 3):
        @pl.when(has[side])
        def _():
            coef_copy(side).wait_send()

        @pl.when(has[5 - side])
        def _():
            coef_copy(side).wait_recv()


def mix_kernel(n, g, rows, depth, pairs, to_off, from_off, term_off, weight, *rest):
    given, (coef, clo, chi, out), rest = rest[:5], rest[5:9], rest[9:]
    held, (sem, shifted, faces), acc = rest[:5], rest[5:8], rest[8:]
    main, ylo, yhi, zlo, zhi = held

    def fetch(i, source):
        return pltpu.make_async_copy(
            given[i].at[source], held[i].at[source], sem.at[i, source])

    @pl.loop(0, n)
    def _(source):
        for i in range(5):
            fetch(i, source).start()

    me, layer = lax.axis_index("modes"), lax.axis_index("gz")
    own = main.shape[1]
    lines = rows * depth
    lanes = main.shape[3]
    terms = coef.shape[0]
    line = lax.broadcasted_iota(jnp.int32, (1, lines, lanes), 1)
    lane = lax.broadcasted_iota(jnp.int32, (1, lines, lanes), 2)
    row, deep = line // depth, line % depth

    def x_shift(value, offset):
        moved = pltpu.roll(value, offset % lanes, 2)
        edge = 0 if offset == 1 else lanes - 1
        return jnp.where(lane == edge, 0.0, moved)

    centre = coef[:, depth:depth + lines, :]
    before, after = clo[:, depth:depth + lines, :], chi[:, depth:depth + lines, :]
    z_before = jnp.where(layer > 0, turn(before, 1 - depth, 1), 0.0)
    z_after = jnp.where(layer < g - 1, turn(after, depth - 1, 1), 0.0)
    around = (
        coef[:, 0:lines, :],
        coef[:, 2 * depth:2 * depth + lines, :],
        jnp.where(deep == 0, z_before, turn(centre, 1, 1)),
        jnp.where(deep == depth - 1, z_after, turn(centre, -1, 1)),
        x_shift(centre, 1),
        x_shift(centre, -1),
    )

    def put_faces(m, value):
        for k in range(terms):
            faces[(k * 7 + m) * lines:(k * 7 + m + 1) * lines, :] = value[k]

    total = None
    for m, other in enumerate(around):
        face = 0.5 * (centre + other)
        put_faces(m + 1, face)
        total = face if total is None else total + face
    put_faces(0, total)

    y_per, y_starts = groups(own, rows)
    z_per, z_starts = groups(own, depth)

    def spans(starts, per):
        seen = 0
        for j, start in enumerate(starts):
            yield j, seen, min(own, start + per), start
            seen = min(own, start + per)

    has = (me > 0, me < n - 1, layer > 0, layer < g - 1)

    def put(base, m, value):
        for i in range(own):
            start = pl.multiple_of(base * (7 * lines), lines) + (i * 7 + m) * lines
            shifted[pl.ds(start, lines), :] = value[i]

    @pl.loop(0, n)
    def _(source):
        for i in range(5):
            fetch(i, source).wait()
        base = source * own
        value = main[source]
        put(base, 0, value)
        put(base, 5, x_shift(value, 1))
        put(base, 6, x_shift(value, -1))

        def edge_pieces(ref, starts, per, wanted, unit, here):
            pieces = []
            for j, first, stop, start in spans(starts, per):
                if stop > first:
                    tile = ref[source, first - start:stop - start]
                    pieces.append(turn(tile, (wanted - j) * unit, 1))
            joined = pieces[0] if len(pieces) == 1 else jnp.concatenate(pieces, axis=0)
            return jnp.where(here, joined, 0.0)

        low = edge_pieces(ylo, y_starts, y_per, 0, depth, has[0])
        high = edge_pieces(yhi, y_starts, y_per, rows - 1, depth, has[1])
        put(base, 1, jnp.where(row == 0, low, turn(value, depth, 1)))
        put(base, 2, jnp.where(row == rows - 1, high, turn(value, -depth, 1)))
        near = edge_pieces(zlo, z_starts, z_per, 0, 1, has[2])
        far = edge_pieces(zhi, z_starts, z_per, depth - 1, 1, has[3])
        put(base, 3, jnp.where(deep == 0, near, turn(value, 1, 1)))
        put(base, 4, jnp.where(deep == depth - 1, far, turn(value, -1, 1)))
        for a in range(ACCS):
            acc[a][pl.ds(pl.multiple_of(base * lines, lines), own * lines), :] = jnp.zeros(
                (own * lines, lanes), jnp.float32)

    def tiles(ref, offset, index):
        return ref[pl.ds(pl.multiple_of(offset, lines) + index * lines, lines), :]

    def add_row(p, a):
        term, source, target = term_off[p], from_off[p], to_off[p]
        part = [tiles(faces, term, m) * tiles(shifted, source, m) for m in range(7)]
        image = (part[0] - (part[1] + part[2])) - ((part[3] + part[4]) + (part[5] + part[6]))
        here = pl.ds(pl.multiple_of(target, lines), lines)
        acc[a][here, :] = acc[a][here, :] + weight[p] * image

    whole = pairs // UNROLL

    @pl.loop(0, whole)
    def _(block):
        for u in range(UNROLL):
            add_row(block * UNROLL + u, u % ACCS)

    for p in range(whole * UNROLL, pairs):
        add_row(p, p % ACCS)

    @pl.loop(0, n)
    def _(source):
        here = pl.ds(pl.multiple_of(source * own * lines, lines), own * lines)
        result = acc[0][here, :]
        for a in range(1, ACCS):
            result = result + acc[a][here, :]
        out[source] = result


def store_kernel(source, out, held, into, back):
    count = source.shape[0]
    for i in range(count):
        pltpu.make_async_copy(source.at[i], held.at[i], into.at[i]).start()
    for i in range(count):
        pltpu.make_async_copy(source.at[i], held.at[i], into.at[i]).wait()
        pltpu.make_async_copy(held.at[i], out.at[i], back.at[i]).start()
    for i in range(count):
        pltpu.make_async_copy(held.at[i], out.at[i], back.at[i]).wait()


def collect_kernel(n, result, out, own_sem, send_sem, recv_sem):
    me, layer = lax.axis_index("modes"), lax.axis_index("gz")
    barrier_with_peers(n, 1)

    sends, waits, plane = step_plan(n)

    def block_copy(step):
        target = partner(me, step, n, plane, 1)
        slot = step[0] * plane + step[1]
        return pltpu.make_async_remote_copy(
            src_ref=result.at[target], dst_ref=out.at[:, me],
            send_sem=send_sem.at[slot], recv_sem=recv_sem.at[slot],
            device_id=(target, layer), device_id_type=pl.DeviceIdType.MESH)

    for step in sends:
        block_copy(step).start()
    mine = pltpu.make_async_copy(result.at[me], out.at[:, me], own_sem)
    mine.start()
    mine.wait()
    for step in waits:
        block_copy(step).wait_recv()
    for step in waits:
        block_copy(step).wait_send()


def body(fields, mean_coeff, random_coeff, coupling, mode_slots):
    n, g = lax.axis_size("modes"), lax.axis_size("gz")
    own, row_total, depth, across = fields.shape
    rows = row_total // n
    lines = rows * depth
    f32 = jnp.float32
    vmem = pl.BlockSpec(memory_space=pltpu.VMEM)
    smem = pl.BlockSpec(memory_space=pltpu.SMEM)
    anywhere = pl.BlockSpec(memory_space=pl.ANY)
    dma = pltpu.SemaphoreType.DMA

    coef = jnp.concatenate([mean_coeff[None], random_coeff], axis=0)
    coef = jnp.pad(coef, ((0, 0), (1, 1), (0, 0), (0, 0)))
    coef = lax.dynamic_slice_in_dim(coef, lax.axis_index("modes") * rows, rows + 2, 1)
    terms = coef.shape[0]
    coef = coef.reshape(terms, (rows + 2) * depth, across)

    degree = jnp.arange(mode_slots.shape[0], dtype=jnp.int32).astype(f32)
    table = (degree + 1.0) / jnp.sqrt((2.0 * degree + 1.0) * (2.0 * degree + 3.0))
    couple = coupling.T
    pairs = couple.shape[1]

    y_per, _ = groups(own, rows)
    z_per, _ = groups(own, depth)
    block = jax.ShapeDtypeStruct((n, own, lines, across), f32)
    y_pack = jax.ShapeDtypeStruct((n, y_per, lines, across), f32)
    z_pack = jax.ShapeDtypeStruct((n, z_per, lines, across), f32)
    offsets = jax.ShapeDtypeStruct((pairs,), jnp.int32)
    coef_like = jax.ShapeDtypeStruct(coef.shape, f32)
    spread = pl.pallas_call(
        functools.partial(spread_kernel, n, g, rows, depth),
        out_shape=(block, y_pack, y_pack, z_pack, z_pack, coef_like, coef_like,
                   offsets, offsets, offsets, jax.ShapeDtypeStruct((pairs,), f32)),
        in_specs=[smem, smem, smem, anywhere, vmem],
        out_specs=[anywhere] * 7 + [smem] * 4,
        scratch_shapes=[
            pltpu.VMEM(block.shape, f32),
            pltpu.VMEM(y_pack.shape, f32), pltpu.VMEM(y_pack.shape, f32),
            pltpu.VMEM(z_pack.shape, f32), pltpu.VMEM(z_pack.shape, f32), dma((n,)),
            dma, dma((n,)), dma((n,)), dma((4, n)), dma((4, n)), dma((2,)), dma((2,)),
        ],
        compiler_params=pltpu.CompilerParams(collective_id=0, has_side_effects=True),
        name="spread",
    )
    received = spread(couple, mode_slots, table, fields.reshape(own, n, lines, across), coef)
    main, ylo, yhi, zlo, zhi, clo, chi, to_off, from_off, term_off, weight = received

    mix = pl.pallas_call(
        functools.partial(mix_kernel, n, g, rows, depth, pairs),
        out_shape=jax.ShapeDtypeStruct((n, own * lines, across), f32),
        in_specs=[smem] * 4 + [anywhere] * 5 + [vmem] * 3,
        out_specs=vmem,
        scratch_shapes=[pltpu.VMEM(a.shape, f32) for a in received[:5]] + [
            dma((5, n)),
            pltpu.VMEM((n * own * 7 * lines, across), f32),
            pltpu.VMEM((terms * 7 * lines, across), f32),
        ] + [pltpu.VMEM((n * own * lines, across), f32)] * ACCS,
        name="mix",
    )
    result = mix(to_off, from_off, term_off, weight, main, ylo, yhi, zlo, zhi, coef, clo, chi)

    collect = pl.pallas_call(
        functools.partial(collect_kernel, n),
        out_shape=jax.ShapeDtypeStruct((own, n, lines, across), f32),
        in_specs=[vmem],
        out_specs=anywhere,
        scratch_shapes=[dma, dma((n,)), dma((n,))],
        compiler_params=pltpu.CompilerParams(collective_id=1, has_side_effects=True),
        name="collect",
    )
    local = (own, n, lines, across)
    store = pl.pallas_call(
        store_kernel,
        out_shape=jax.ShapeDtypeStruct(local, f32),
        in_specs=[anywhere],
        out_specs=anywhere,
        scratch_shapes=[pltpu.VMEM(local, f32), dma((own,)), dma((own,))],
        name="store",
    )
    return store(collect(result.reshape(block.shape))).reshape(fields.shape)


def solution(mesh):
    in_specs = (
        P("modes", None, "gz", None),
        P(None, "gz", None),
        P(None, None, "gz", None),
        P(),
        P(),
    )
    out_specs = P("modes", None, "gz", None)
    return jax.shard_map(body, mesh=mesh, in_specs=in_specs, out_specs=out_specs, check_vma=False)
```

```python
import functools

import jax
import jax.numpy as jnp
from jax import lax
from jax.experimental import pallas as pl
from jax.experimental.pallas import tpu as pltpu
from jax.sharding import PartitionSpec as P

ACCS = 2
UNROLL = 73


def turn(value, shift, axis):
    size = value.shape[axis]
    shift %= size
    if shift == 0:
        return value
    low = lax.slice_in_dim(value, size - shift, size, axis=axis)
    high = lax.slice_in_dim(value, 0, size - shift, axis=axis)
    return jnp.concatenate([low, high], axis=axis)


def step_plan(count):
    plane = max(p for p in range(1, count + 1) if count % p == 0 and p * p <= count)
    planes = count // plane
    far = sorted(range(1, planes), key=lambda d: (abs(d - planes // 2), d))
    near = [(0, j) for j in range(1, plane)]
    away = [(d, j) for d in far for j in range(plane)]
    return away + near, near + away, plane


def partner(me, step, count, plane, sign):
    planes = count // plane
    outer = lax.rem(me // plane + planes + sign * step[0], planes)
    inner = lax.rem(lax.rem(me, plane) + plane + sign * step[1], plane)
    return outer * plane + inner


def groups(own, parts):
    per = -(-own // parts)
    return per, [min(j * per, own - per) for j in range(parts)]


def barrier_with_peers(peers_modes, peers_gz):
    me, layer = lax.axis_index("modes"), lax.axis_index("gz")
    barrier = pltpu.get_barrier_semaphore()

    @pl.loop(1, peers_modes)
    def _(step):
        pl.semaphore_signal(
            barrier, inc=1, device_id=(lax.rem(me + step, peers_modes), layer),
            device_id_type=pl.DeviceIdType.MESH)

    @pl.loop(1, peers_gz)
    def _(step):
        pl.semaphore_signal(
            barrier, inc=1, device_id=(me, lax.rem(layer + step, peers_gz)),
            device_id_type=pl.DeviceIdType.MESH)

    pl.semaphore_wait(barrier, peers_modes + peers_gz - 2)


def spread_kernel(n, g, rows, depth, couple, slots, table, fields, coef,
                  main_out, ylo, yhi, zlo, zhi, clo, chi, to_off, from_off, term_off, weight,
                  main, ylo_out, yhi_out, zlo_out, zhi_out, out_sem,
                  own_sem, send_sem, recv_sem, halo_send, halo_recv, coef_send, coef_recv):
    me, layer = lax.axis_index("modes"), lax.axis_index("gz")
    own = fields.shape[0]
    lines = rows * depth
    mesh_id = pl.DeviceIdType.MESH
    has = (me > 0, me < n - 1, layer > 0, layer < g - 1)
    to = ((me - 1, layer), (me + 1, layer), (me, layer - 1), (me, layer + 1))
    packed = (ylo_out, yhi_out, zlo_out, zhi_out)
    landing = (yhi, ylo, zhi, zlo)
    barrier_with_peers(n, g)

    _, sends, plane = step_plan(n)
    waits = sends

    def block_copy(step):
        target = partner(me, step, n, plane, 1)
        slot = step[0] * plane + step[1]
        return pltpu.make_async_remote_copy(
            src_ref=fields.at[:, target], dst_ref=main.at[me],
            send_sem=send_sem.at[slot], recv_sem=recv_sem.at[slot],
            device_id=(target, layer), device_id_type=mesh_id)

    def coef_copy(side):
        return pltpu.make_async_remote_copy(
            src_ref=coef, dst_ref=(chi, clo)[side - 2],
            send_sem=coef_send.at[side - 2], recv_sem=coef_recv.at[side - 2],
            device_id=to[side], device_id_type=mesh_id)

    def halo_copy(side, source):
        return pltpu.make_async_remote_copy(
            src_ref=packed[side].at[source], dst_ref=landing[side].at[source],
            send_sem=halo_send.at[side, source], recv_sem=halo_recv.at[side, source],
            device_id=to[side], device_id_type=mesh_id)

    for step in sends:
        block_copy(step).start()
    mine = pltpu.make_async_copy(fields.at[:, me], main.at[me], own_sem)
    mine.start()
    for side in (2, 3):
        @pl.when(has[side])
        def _():
            coef_copy(side).start()

    y_per, y_starts = groups(own, rows)
    z_per, z_starts = groups(own, depth)

    pairs = couple.shape[1]
    share = -(-pairs // n)

    def decode(part):
        @pl.loop(part * share, min(pairs, (part + 1) * share))
        def _(p):
            term = couple[2, p]
            to_off[p] = slots[couple[0, p]] * lines
            from_off[p] = slots[couple[1, p]] * (7 * lines)
            term_off[p] = term * (7 * lines)
            weight[p] = jnp.where(term == 0, jnp.float32(1.0), table[couple[3, p]])

    def pack(source):
        line = lax.broadcasted_iota(jnp.int32, (1, lines, 1), 1)
        for out, edge in ((ylo_out, 0), (yhi_out, rows - 1)):
            tile = None
            for j, start in enumerate(y_starts):
                part = turn(main[source, start:start + y_per], (j - edge) * depth, 1)
                tile = part if tile is None else jnp.where(line // depth == j, part, tile)
            out[source] = tile
        for out, edge in ((zlo_out, 0), (zhi_out, depth - 1)):
            tile = None
            for j, start in enumerate(z_starts):
                part = turn(main[source, start:start + z_per], j - edge, 1)
                tile = part if tile is None else jnp.where(line % depth == j, part, tile)
            out[source] = tile

    def keep(source):
        return pltpu.make_async_copy(main.at[source], main_out.at[source], out_sem.at[source])

    def send_halo(source):
        for side in range(4):
            @pl.when(has[side])
            def _():
                halo_copy(side, source).start()

    decode(0)
    mine.wait()
    keep(me).start()
    pack(me)
    previous = me
    for part, step in enumerate(waits):
        source = partner(me, step, n, plane, -1)
        block_copy(step).wait_recv()
        keep(source).start()
        send_halo(previous)
        pack(source)
        decode(part + 1)
        previous = source
    for step in sends:
        block_copy(step).wait_send()
    send_halo(previous)

    @pl.loop(0, n)
    def _(source):
        keep(source).wait()

    for side in range(4):
        @pl.when(has[side])
        def _():
            @pl.loop(0, n)
            def _(source):
                halo_copy(side, source).wait_send()

        opposite = (1, 0, 3, 2)[side]

        @pl.when(has[opposite])
        def _():
            @pl.loop(0, n)
            def _(source):
                halo_copy(side, source).wait_recv()
    for side in (2, 3):
        @pl.when(has[side])
        def _():
            coef_copy(side).wait_send()

        @pl.when(has[5 - side])
        def _():
            coef_copy(side).wait_recv()


def mix_kernel(n, g, rows, depth, pairs, to_off, from_off, term_off, weight, *rest):
    given, (coef, clo, chi, out), rest = rest[:5], rest[5:9], rest[9:]
    held, (sem, shifted, faces), acc = rest[:5], rest[5:8], rest[8:]
    main, ylo, yhi, zlo, zhi = held

    def fetch(i, source):
        return pltpu.make_async_copy(
            given[i].at[source], held[i].at[source], sem.at[i, source])

    @pl.loop(0, n)
    def _(source):
        for i in range(5):
            fetch(i, source).start()

    me, layer = lax.axis_index("modes"), lax.axis_index("gz")
    own = main.shape[1]
    lines = rows * depth
    lanes = main.shape[3]
    terms = coef.shape[0]
    line = lax.broadcasted_iota(jnp.int32, (1, lines, lanes), 1)
    lane = lax.broadcasted_iota(jnp.int32, (1, lines, lanes), 2)
    row, deep = line // depth, line % depth

    def x_shift(value, offset):
        moved = pltpu.roll(value, offset % lanes, 2)
        edge = 0 if offset == 1 else lanes - 1
        return jnp.where(lane == edge, 0.0, moved)

    centre = coef[:, depth:depth + lines, :]
    before, after = clo[:, depth:depth + lines, :], chi[:, depth:depth + lines, :]
    z_before = jnp.where(layer > 0, turn(before, 1 - depth, 1), 0.0)
    z_after = jnp.where(layer < g - 1, turn(after, depth - 1, 1), 0.0)
    around = (
        coef[:, 0:lines, :],
        coef[:, 2 * depth:2 * depth + lines, :],
        jnp.where(deep == 0, z_before, turn(centre, 1, 1)),
        jnp.where(deep == depth - 1, z_after, turn(centre, -1, 1)),
        x_shift(centre, 1),
        x_shift(centre, -1),
    )

    def put_faces(m, value):
        for k in range(terms):
            faces[(k * 7 + m) * lines:(k * 7 + m + 1) * lines, :] = value[k]

    total = None
    for m, other in enumerate(around):
        face = 0.5 * (centre + other)
        put_faces(m + 1, face)
        total = face if total is None else total + face
    put_faces(0, total)

    y_per, y_starts = groups(own, rows)
    z_per, z_starts = groups(own, depth)

    def spans(starts, per):
        seen = 0
        for j, start in enumerate(starts):
            yield j, seen, min(own, start + per), start
            seen = min(own, start + per)

    has = (me > 0, me < n - 1, layer > 0, layer < g - 1)

    def put(base, m, value):
        for i in range(own):
            start = pl.multiple_of(base * (7 * lines), lines) + (i * 7 + m) * lines
            shifted[pl.ds(start, lines), :] = value[i]

    @pl.loop(0, n)
    def _(source):
        for i in range(5):
            fetch(i, source).wait()
        base = source * own
        value = main[source]
        put(base, 0, value)
        put(base, 5, x_shift(value, 1))
        put(base, 6, x_shift(value, -1))

        def edge_pieces(ref, starts, per, wanted, unit, here):
            pieces = []
            for j, first, stop, start in spans(starts, per):
                if stop > first:
                    tile = ref[source, first - start:stop - start]
                    pieces.append(turn(tile, (wanted - j) * unit, 1))
            joined = pieces[0] if len(pieces) == 1 else jnp.concatenate(pieces, axis=0)
            return jnp.where(here, joined, 0.0)

        low = edge_pieces(ylo, y_starts, y_per, 0, depth, has[0])
        high = edge_pieces(yhi, y_starts, y_per, rows - 1, depth, has[1])
        put(base, 1, jnp.where(row == 0, low, turn(value, depth, 1)))
        put(base, 2, jnp.where(row == rows - 1, high, turn(value, -depth, 1)))
        near = edge_pieces(zlo, z_starts, z_per, 0, 1, has[2])
        far = edge_pieces(zhi, z_starts, z_per, depth - 1, 1, has[3])
        put(base, 3, jnp.where(deep == 0, near, turn(value, 1, 1)))
        put(base, 4, jnp.where(deep == depth - 1, far, turn(value, -1, 1)))
        for a in range(ACCS):
            acc[a][pl.ds(pl.multiple_of(base * lines, lines), own * lines), :] = jnp.zeros(
                (own * lines, lanes), jnp.float32)

    def tiles(ref, offset, index):
        return ref[pl.ds(pl.multiple_of(offset, lines) + index * lines, lines), :]

    def add_row(p, a):
        term, source, target = term_off[p], from_off[p], to_off[p]
        part = [tiles(faces, term, m) * tiles(shifted, source, m) for m in range(7)]
        image = (part[0] - (part[1] + part[2])) - ((part[3] + part[4]) + (part[5] + part[6]))
        here = pl.ds(pl.multiple_of(target, lines), lines)
        acc[a][here, :] = acc[a][here, :] + weight[p] * image

    whole = pairs // UNROLL

    @pl.loop(0, whole)
    def _(block):
        for u in range(UNROLL):
            add_row(block * UNROLL + u, u % ACCS)

    for p in range(whole * UNROLL, pairs):
        add_row(p, p % ACCS)

    @pl.loop(0, n)
    def _(source):
        here = pl.ds(pl.multiple_of(source * own * lines, lines), own * lines)
        result = acc[0][here, :]
        for a in range(1, ACCS):
            result = result + acc[a][here, :]
        out[source] = result


def store_kernel(source, out, held, into, back):
    count = source.shape[0]
    for i in range(count):
        pltpu.make_async_copy(source.at[i], held.at[i], into.at[i]).start()
    for i in range(count):
        pltpu.make_async_copy(source.at[i], held.at[i], into.at[i]).wait()
        pltpu.make_async_copy(held.at[i], out.at[i], back.at[i]).start()
    for i in range(count):
        pltpu.make_async_copy(held.at[i], out.at[i], back.at[i]).wait()


def collect_kernel(n, result, out, own_sem, send_sem, recv_sem):
    me, layer = lax.axis_index("modes"), lax.axis_index("gz")
    barrier_with_peers(n, 1)

    sends, waits, plane = step_plan(n)

    def block_copy(step):
        target = partner(me, step, n, plane, 1)
        slot = step[0] * plane + step[1]
        return pltpu.make_async_remote_copy(
            src_ref=result.at[target], dst_ref=out.at[:, me],
            send_sem=send_sem.at[slot], recv_sem=recv_sem.at[slot],
            device_id=(target, layer), device_id_type=pl.DeviceIdType.MESH)

    for step in sends:
        block_copy(step).start()
    mine = pltpu.make_async_copy(result.at[me], out.at[:, me], own_sem)
    mine.start()
    mine.wait()
    for step in waits:
        block_copy(step).wait_recv()
    for step in waits:
        block_copy(step).wait_send()


def body(fields, mean_coeff, random_coeff, coupling, mode_slots):
    n, g = lax.axis_size("modes"), lax.axis_size("gz")
    own, row_total, depth, across = fields.shape
    rows = row_total // n
    lines = rows * depth
    f32 = jnp.float32
    vmem = pl.BlockSpec(memory_space=pltpu.VMEM)
    smem = pl.BlockSpec(memory_space=pltpu.SMEM)
    anywhere = pl.BlockSpec(memory_space=pl.ANY)
    dma = pltpu.SemaphoreType.DMA

    coef = jnp.concatenate([mean_coeff[None], random_coeff], axis=0)
    coef = jnp.pad(coef, ((0, 0), (1, 1), (0, 0), (0, 0)))
    coef = lax.dynamic_slice_in_dim(coef, lax.axis_index("modes") * rows, rows + 2, 1)
    terms = coef.shape[0]
    coef = coef.reshape(terms, (rows + 2) * depth, across)

    degree = jnp.arange(mode_slots.shape[0], dtype=jnp.int32).astype(f32)
    table = (degree + 1.0) / jnp.sqrt((2.0 * degree + 1.0) * (2.0 * degree + 3.0))
    couple = coupling.T
    pairs = couple.shape[1]

    y_per, _ = groups(own, rows)
    z_per, _ = groups(own, depth)
    block = jax.ShapeDtypeStruct((n, own, lines, across), f32)
    y_pack = jax.ShapeDtypeStruct((n, y_per, lines, across), f32)
    z_pack = jax.ShapeDtypeStruct((n, z_per, lines, across), f32)
    offsets = jax.ShapeDtypeStruct((pairs,), jnp.int32)
    coef_like = jax.ShapeDtypeStruct(coef.shape, f32)
    spread = pl.pallas_call(
        functools.partial(spread_kernel, n, g, rows, depth),
        out_shape=(block, y_pack, y_pack, z_pack, z_pack, coef_like, coef_like,
                   offsets, offsets, offsets, jax.ShapeDtypeStruct((pairs,), f32)),
        in_specs=[smem, smem, smem, anywhere, vmem],
        out_specs=[anywhere] * 7 + [smem] * 4,
        scratch_shapes=[
            pltpu.VMEM(block.shape, f32),
            pltpu.VMEM(y_pack.shape, f32), pltpu.VMEM(y_pack.shape, f32),
            pltpu.VMEM(z_pack.shape, f32), pltpu.VMEM(z_pack.shape, f32), dma((n,)),
            dma, dma((n,)), dma((n,)), dma((4, n)), dma((4, n)), dma((2,)), dma((2,)),
        ],
        compiler_params=pltpu.CompilerParams(collective_id=0, has_side_effects=True),
        name="spread",
    )
    received = spread(couple, mode_slots, table, fields.reshape(own, n, lines, across), coef)
    main, ylo, yhi, zlo, zhi, clo, chi, to_off, from_off, term_off, weight = received

    mix = pl.pallas_call(
        functools.partial(mix_kernel, n, g, rows, depth, pairs),
        out_shape=jax.ShapeDtypeStruct((n, own * lines, across), f32),
        in_specs=[smem] * 4 + [anywhere] * 5 + [vmem] * 3,
        out_specs=vmem,
        scratch_shapes=[pltpu.VMEM(a.shape, f32) for a in received[:5]] + [
            dma((5, n)),
            pltpu.VMEM((n * own * 7 * lines, across), f32),
            pltpu.VMEM((terms * 7 * lines, across), f32),
        ] + [pltpu.VMEM((n * own * lines, across), f32)] * ACCS,
        name="mix",
    )
    result = mix(to_off, from_off, term_off, weight, main, ylo, yhi, zlo, zhi, coef, clo, chi)

    collect = pl.pallas_call(
        functools.partial(collect_kernel, n),
        out_shape=jax.ShapeDtypeStruct((own, n, lines, across), f32),
        in_specs=[vmem],
        out_specs=anywhere,
        scratch_shapes=[dma, dma((n,)), dma((n,))],
        compiler_params=pltpu.CompilerParams(collective_id=1, has_side_effects=True),
        name="collect",
    )
    local = (own, n, lines, across)
    store = pl.pallas_call(
        store_kernel,
        out_shape=jax.ShapeDtypeStruct(local, f32),
        in_specs=[anywhere],
        out_specs=anywhere,
        scratch_shapes=[pltpu.VMEM(local, f32), dma((own,)), dma((own,))],
        name="store",
    )
    return store(collect(result.reshape(block.shape))).reshape(fields.shape)


def solution(mesh):
    in_specs = (
        P("modes", None, "gz", None),
        P(None, "gz", None),
        P(None, None, "gz", None),
        P(),
        P(),
    )
    out_specs = P("modes", None, "gz", None)
    return jax.shard_map(body, mesh=mesh, in_specs=in_specs, out_specs=out_specs, check_vma=False)
```

```python
import functools

import jax
import jax.numpy as jnp
from jax import lax
from jax.experimental import pallas as pl
from jax.experimental.pallas import tpu as pltpu
from jax.sharding import PartitionSpec as P

ACCS = 2
UNROLL = 73


def turn(value, shift, axis):
    size = value.shape[axis]
    shift %= size
    if shift == 0:
        return value
    low = lax.slice_in_dim(value, size - shift, size, axis=axis)
    high = lax.slice_in_dim(value, 0, size - shift, axis=axis)
    return jnp.concatenate([low, high], axis=axis)


def step_plan(count):
    plane = max(p for p in range(1, count + 1) if count % p == 0 and p * p <= count)
    planes = count // plane
    far = sorted(range(1, planes), key=lambda d: (abs(d - planes // 2), d))
    near = [(0, j) for j in range(1, plane)]
    away = [(d, j) for d in far for j in range(plane)]
    return away + near, near + away, plane


def partner(me, step, count, plane, sign):
    planes = count // plane
    outer = lax.rem(me // plane + planes + sign * step[0], planes)
    inner = lax.rem(lax.rem(me, plane) + plane + sign * step[1], plane)
    return outer * plane + inner


def groups(own, parts):
    per = -(-own // parts)
    return per, [min(j * per, own - per) for j in range(parts)]


def barrier_with_peers(peers_modes, peers_gz):
    me, layer = lax.axis_index("modes"), lax.axis_index("gz")
    barrier = pltpu.get_barrier_semaphore()

    @pl.loop(1, peers_modes)
    def _(step):
        pl.semaphore_signal(
            barrier, inc=1, device_id=(lax.rem(me + step, peers_modes), layer),
            device_id_type=pl.DeviceIdType.MESH)

    @pl.loop(1, peers_gz)
    def _(step):
        pl.semaphore_signal(
            barrier, inc=1, device_id=(me, lax.rem(layer + step, peers_gz)),
            device_id_type=pl.DeviceIdType.MESH)

    pl.semaphore_wait(barrier, peers_modes + peers_gz - 2)


def spread_kernel(n, g, rows, depth, couple, slots, table, fields, coef,
                  main_out, ylo, yhi, zlo, zhi, clo, chi, to_off, from_off, term_off, weight,
                  main, ylo_out, yhi_out, zlo_out, zhi_out, out_sem,
                  own_sem, send_sem, recv_sem, halo_send, halo_recv, coef_send, coef_recv):
    me, layer = lax.axis_index("modes"), lax.axis_index("gz")
    own = fields.shape[0]
    lines = rows * depth
    mesh_id = pl.DeviceIdType.MESH
    has = (me > 0, me < n - 1, layer > 0, layer < g - 1)
    to = ((me - 1, layer), (me + 1, layer), (me, layer - 1), (me, layer + 1))
    packed = (ylo_out, yhi_out, zlo_out, zhi_out)
    landing = (yhi, ylo, zhi, zlo)
    barrier_with_peers(n, g)

    sends = sorted(range(1, n), key=lambda d: (abs(d - n // 2), d))
    waits = sends

    def block_copy(slot):
        target = lax.rem(me + slot, n)
        return pltpu.make_async_remote_copy(
            src_ref=fields.at[:, target], dst_ref=main.at[me],
            send_sem=send_sem.at[slot], recv_sem=recv_sem.at[slot],
            device_id=(target, layer), device_id_type=mesh_id)

    def coef_copy(side):
        return pltpu.make_async_remote_copy(
            src_ref=coef, dst_ref=(chi, clo)[side - 2],
            send_sem=coef_send.at[side - 2], recv_sem=coef_recv.at[side - 2],
            device_id=to[side], device_id_type=mesh_id)

    def halo_copy(side, source):
        return pltpu.make_async_remote_copy(
            src_ref=packed[side].at[source], dst_ref=landing[side].at[source],
            send_sem=halo_send.at[side, source], recv_sem=halo_recv.at[side, source],
            device_id=to[side], device_id_type=mesh_id)

    for step in sends:
        block_copy(step).start()
    mine = pltpu.make_async_copy(fields.at[:, me], main.at[me], own_sem)
    mine.start()
    for side in (2, 3):
        @pl.when(has[side])
        def _():
            coef_copy(side).start()

    y_per, y_starts = groups(own, rows)
    z_per, z_starts = groups(own, depth)

    pairs = couple.shape[1]
    share = -(-pairs // n)

    def decode(part):
        @pl.loop(part * share, min(pairs, (part + 1) * share))
        def _(p):
            term = couple[2, p]
            to_off[p] = slots[couple[0, p]] * lines
            from_off[p] = slots[couple[1, p]] * (7 * lines)
            term_off[p] = term * (7 * lines)
            weight[p] = jnp.where(term == 0, jnp.float32(1.0), table[couple[3, p]])

    def pack(source):
        line = lax.broadcasted_iota(jnp.int32, (1, lines, 1), 1)
        for out, edge in ((ylo_out, 0), (yhi_out, rows - 1)):
            tile = None
            for j, start in enumerate(y_starts):
                part = turn(main[source, start:start + y_per], (j - edge) * depth, 1)
                tile = part if tile is None else jnp.where(line // depth == j, part, tile)
            out[source] = tile
        for out, edge in ((zlo_out, 0), (zhi_out, depth - 1)):
            tile = None
            for j, start in enumerate(z_starts):
                part = turn(main[source, start:start + z_per], j - edge, 1)
                tile = part if tile is None else jnp.where(line % depth == j, part, tile)
            out[source] = tile

    def keep(source):
        return pltpu.make_async_copy(main.at[source], main_out.at[source], out_sem.at[source])

    def send_halo(source):
        for side in range(4):
            @pl.when(has[side])
            def _():
                halo_copy(side, source).start()

    decode(0)
    mine.wait()
    keep(me).start()
    pack(me)
    previous = me
    for part, step in enumerate(waits):
        source = lax.rem(me + n - step, n)
        block_copy(step).wait_recv()
        keep(source).start()
        send_halo(previous)
        pack(source)
        decode(part + 1)
        previous = source
    for step in sends:
        block_copy(step).wait_send()
    send_halo(previous)

    @pl.loop(0, n)
    def _(source):
        keep(source).wait()

    for side in range(4):
        @pl.when(has[side])
        def _():
            @pl.loop(0, n)
            def _(source):
                halo_copy(side, source).wait_send()

        opposite = (1, 0, 3, 2)[side]

        @pl.when(has[opposite])
        def _():
            @pl.loop(0, n)
            def _(source):
                halo_copy(side, source).wait_recv()
    for side in (2, 3):
        @pl.when(has[side])
        def _():
            coef_copy(side).wait_send()

        @pl.when(has[5 - side])
        def _():
            coef_copy(side).wait_recv()


def mix_kernel(n, g, rows, depth, pairs, to_off, from_off, term_off, weight, *rest):
    given, (coef, clo, chi, out), rest = rest[:5], rest[5:9], rest[9:]
    held, (sem, shifted, faces), acc = rest[:5], rest[5:8], rest[8:]
    main, ylo, yhi, zlo, zhi = held

    def fetch(i, source):
        return pltpu.make_async_copy(
            given[i].at[source], held[i].at[source], sem.at[i, source])

    @pl.loop(0, n)
    def _(source):
        for i in range(5):
            fetch(i, source).start()

    me, layer = lax.axis_index("modes"), lax.axis_index("gz")
    own = main.shape[1]
    lines = rows * depth
    lanes = main.shape[3]
    terms = coef.shape[0]
    line = lax.broadcasted_iota(jnp.int32, (1, lines, lanes), 1)
    lane = lax.broadcasted_iota(jnp.int32, (1, lines, lanes), 2)
    row, deep = line // depth, line % depth

    def x_shift(value, offset):
        moved = pltpu.roll(value, offset % lanes, 2)
        edge = 0 if offset == 1 else lanes - 1
        return jnp.where(lane == edge, 0.0, moved)

    centre = coef[:, depth:depth + lines, :]
    before, after = clo[:, depth:depth + lines, :], chi[:, depth:depth + lines, :]
    z_before = jnp.where(layer > 0, turn(before, 1 - depth, 1), 0.0)
    z_after = jnp.where(layer < g - 1, turn(after, depth - 1, 1), 0.0)
    around = (
        coef[:, 0:lines, :],
        coef[:, 2 * depth:2 * depth + lines, :],
        jnp.where(deep == 0, z_before, turn(centre, 1, 1)),
        jnp.where(deep == depth - 1, z_after, turn(centre, -1, 1)),
        x_shift(centre, 1),
        x_shift(centre, -1),
    )

    def put_faces(m, value):
        for k in range(terms):
            faces[(k * 7 + m) * lines:(k * 7 + m + 1) * lines, :] = value[k]

    total = None
    for m, other in enumerate(around):
        face = 0.5 * (centre + other)
        put_faces(m + 1, face)
        total = face if total is None else total + face
    put_faces(0, total)

    y_per, y_starts = groups(own, rows)
    z_per, z_starts = groups(own, depth)

    def spans(starts, per):
        seen = 0
        for j, start in enumerate(starts):
            yield j, seen, min(own, start + per), start
            seen = min(own, start + per)

    has = (me > 0, me < n - 1, layer > 0, layer < g - 1)

    def put(base, m, value):
        for i in range(own):
            start = pl.multiple_of(base * (7 * lines), lines) + (i * 7 + m) * lines
            shifted[pl.ds(start, lines), :] = value[i]

    @pl.loop(0, n)
    def _(source):
        for i in range(5):
            fetch(i, source).wait()
        base = source * own
        value = main[source]
        put(base, 0, value)
        put(base, 5, x_shift(value, 1))
        put(base, 6, x_shift(value, -1))

        def edge_pieces(ref, starts, per, wanted, unit, here):
            pieces = []
            for j, first, stop, start in spans(starts, per):
                if stop > first:
                    tile = ref[source, first - start:stop - start]
                    pieces.append(turn(tile, (wanted - j) * unit, 1))
            joined = pieces[0] if len(pieces) == 1 else jnp.concatenate(pieces, axis=0)
            return jnp.where(here, joined, 0.0)

        low = edge_pieces(ylo, y_starts, y_per, 0, depth, has[0])
        high = edge_pieces(yhi, y_starts, y_per, rows - 1, depth, has[1])
        put(base, 1, jnp.where(row == 0, low, turn(value, depth, 1)))
        put(base, 2, jnp.where(row == rows - 1, high, turn(value, -depth, 1)))
        near = edge_pieces(zlo, z_starts, z_per, 0, 1, has[2])
        far = edge_pieces(zhi, z_starts, z_per, depth - 1, 1, has[3])
        put(base, 3, jnp.where(deep == 0, near, turn(value, 1, 1)))
        put(base, 4, jnp.where(deep == depth - 1, far, turn(value, -1, 1)))
        for a in range(ACCS):
            acc[a][pl.ds(pl.multiple_of(base * lines, lines), own * lines), :] = jnp.zeros(
                (own * lines, lanes), jnp.float32)

    def tiles(ref, offset, index):
        return ref[pl.ds(pl.multiple_of(offset, lines) + index * lines, lines), :]

    def add_row(p, a):
        term, source, target = term_off[p], from_off[p], to_off[p]
        part = [tiles(faces, term, m) * tiles(shifted, source, m) for m in range(7)]
        image = (part[0] - (part[1] + part[2])) - ((part[3] + part[4]) + (part[5] + part[6]))
        here = pl.ds(pl.multiple_of(target, lines), lines)
        acc[a][here, :] = acc[a][here, :] + weight[p] * image

    whole = pairs // UNROLL

    @pl.loop(0, whole)
    def _(block):
        for u in range(UNROLL):
            add_row(block * UNROLL + u, u % ACCS)

    for p in range(whole * UNROLL, pairs):
        add_row(p, p % ACCS)

    @pl.loop(0, n)
    def _(source):
        here = pl.ds(pl.multiple_of(source * own * lines, lines), own * lines)
        result = acc[0][here, :]
        for a in range(1, ACCS):
            result = result + acc[a][here, :]
        out[source] = result


def store_kernel(source, out, held, into, back):
    count = source.shape[0]
    for i in range(count):
        pltpu.make_async_copy(source.at[i], held.at[i], into.at[i]).start()
    for i in range(count):
        pltpu.make_async_copy(source.at[i], held.at[i], into.at[i]).wait()
        pltpu.make_async_copy(held.at[i], out.at[i], back.at[i]).start()
    for i in range(count):
        pltpu.make_async_copy(held.at[i], out.at[i], back.at[i]).wait()


def collect_kernel(n, result, out, own_sem, send_sem, recv_sem):
    me, layer = lax.axis_index("modes"), lax.axis_index("gz")
    barrier_with_peers(n, 1)

    sends, waits, plane = step_plan(n)

    def block_copy(step):
        target = partner(me, step, n, plane, 1)
        slot = step[0] * plane + step[1]
        return pltpu.make_async_remote_copy(
            src_ref=result.at[target], dst_ref=out.at[:, me],
            send_sem=send_sem.at[slot], recv_sem=recv_sem.at[slot],
            device_id=(target, layer), device_id_type=pl.DeviceIdType.MESH)

    for step in sends:
        block_copy(step).start()
    mine = pltpu.make_async_copy(result.at[me], out.at[:, me], own_sem)
    mine.start()
    mine.wait()
    for step in waits:
        block_copy(step).wait_recv()
    for step in waits:
        block_copy(step).wait_send()


def body(fields, mean_coeff, random_coeff, coupling, mode_slots):
    n, g = lax.axis_size("modes"), lax.axis_size("gz")
    own, row_total, depth, across = fields.shape
    rows = row_total // n
    lines = rows * depth
    f32 = jnp.float32
    vmem = pl.BlockSpec(memory_space=pltpu.VMEM)
    smem = pl.BlockSpec(memory_space=pltpu.SMEM)
    anywhere = pl.BlockSpec(memory_space=pl.ANY)
    dma = pltpu.SemaphoreType.DMA

    coef = jnp.concatenate([mean_coeff[None], random_coeff], axis=0)
    coef = jnp.pad(coef, ((0, 0), (1, 1), (0, 0), (0, 0)))
    coef = lax.dynamic_slice_in_dim(coef, lax.axis_index("modes") * rows, rows + 2, 1)
    terms = coef.shape[0]
    coef = coef.reshape(terms, (rows + 2) * depth, across)

    degree = jnp.arange(mode_slots.shape[0], dtype=jnp.int32).astype(f32)
    table = (degree + 1.0) / jnp.sqrt((2.0 * degree + 1.0) * (2.0 * degree + 3.0))
    couple = coupling.T
    pairs = couple.shape[1]

    y_per, _ = groups(own, rows)
    z_per, _ = groups(own, depth)
    block = jax.ShapeDtypeStruct((n, own, lines, across), f32)
    y_pack = jax.ShapeDtypeStruct((n, y_per, lines, across), f32)
    z_pack = jax.ShapeDtypeStruct((n, z_per, lines, across), f32)
    offsets = jax.ShapeDtypeStruct((pairs,), jnp.int32)
    coef_like = jax.ShapeDtypeStruct(coef.shape, f32)
    spread = pl.pallas_call(
        functools.partial(spread_kernel, n, g, rows, depth),
        out_shape=(block, y_pack, y_pack, z_pack, z_pack, coef_like, coef_like,
                   offsets, offsets, offsets, jax.ShapeDtypeStruct((pairs,), f32)),
        in_specs=[smem, smem, smem, anywhere, vmem],
        out_specs=[anywhere] * 7 + [smem] * 4,
        scratch_shapes=[
            pltpu.VMEM(block.shape, f32),
            pltpu.VMEM(y_pack.shape, f32), pltpu.VMEM(y_pack.shape, f32),
            pltpu.VMEM(z_pack.shape, f32), pltpu.VMEM(z_pack.shape, f32), dma((n,)),
            dma, dma((n,)), dma((n,)), dma((4, n)), dma((4, n)), dma((2,)), dma((2,)),
        ],
        compiler_params=pltpu.CompilerParams(collective_id=0, has_side_effects=True),
        name="spread",
    )
    received = spread(couple, mode_slots, table, fields.reshape(own, n, lines, across), coef)
    main, ylo, yhi, zlo, zhi, clo, chi, to_off, from_off, term_off, weight = received

    mix = pl.pallas_call(
        functools.partial(mix_kernel, n, g, rows, depth, pairs),
        out_shape=jax.ShapeDtypeStruct((n, own * lines, across), f32),
        in_specs=[smem] * 4 + [anywhere] * 5 + [vmem] * 3,
        out_specs=vmem,
        scratch_shapes=[pltpu.VMEM(a.shape, f32) for a in received[:5]] + [
            dma((5, n)),
            pltpu.VMEM((n * own * 7 * lines, across), f32),
            pltpu.VMEM((terms * 7 * lines, across), f32),
        ] + [pltpu.VMEM((n * own * lines, across), f32)] * ACCS,
        name="mix",
    )
    result = mix(to_off, from_off, term_off, weight, main, ylo, yhi, zlo, zhi, coef, clo, chi)

    collect = pl.pallas_call(
        functools.partial(collect_kernel, n),
        out_shape=jax.ShapeDtypeStruct((own, n, lines, across), f32),
        in_specs=[vmem],
        out_specs=anywhere,
        scratch_shapes=[dma, dma((n,)), dma((n,))],
        compiler_params=pltpu.CompilerParams(collective_id=1, has_side_effects=True),
        name="collect",
    )
    local = (own, n, lines, across)
    store = pl.pallas_call(
        store_kernel,
        out_shape=jax.ShapeDtypeStruct(local, f32),
        in_specs=[anywhere],
        out_specs=anywhere,
        scratch_shapes=[pltpu.VMEM(local, f32), dma((own,)), dma((own,))],
        name="store",
    )
    return store(collect(result.reshape(block.shape))).reshape(fields.shape)


def solution(mesh):
    in_specs = (
        P("modes", None, "gz", None),
        P(None, "gz", None),
        P(None, None, "gz", None),
        P(),
        P(),
    )
    out_specs = P("modes", None, "gz", None)
    return jax.shard_map(body, mesh=mesh, in_specs=in_specs, out_specs=out_specs, check_vma=False)
```
